32 devices in a mesh: expert: 8 (over z, x), half: 4 (over y, core).
Axes of the slice: x: 2, y: 2, z: 4, core: 2. Of those that a mesh axis runs over, the one named last changes fastest.
Arguments:
- tokens: bfloat16 [1024, 2048], P('expert'), may hold values from -6 to 6
- out_grad: bfloat16 [1024, 2048], P('expert'), may hold values from -6 to 6
- assign: int32 [1024, 8], P('expert'), may hold values from 0 to 15, all different within a row; in each aligned block of 128 rows (0 to 127, 128 to 255, ...) at most 64 rows name the same one
- gate_weights: bfloat16 [1024, 8], P('expert'), may hold values from 0.099609375 to 1
- w_gate: bfloat16 [16, 768, 2048], P('expert', 'half'), may hold values from -0.125 to 0.125
- w_up: bfloat16 [16, 768, 2048], P('expert', 'half'), may hold values from -0.125 to 0.125
- w_down: bfloat16 [16, 768, 2048], P('expert', 'half'), may hold values from -0.21875 to 0.21875
Outputs:
- input_grad: bfloat16 [1024, 2048], P(('expert', 'half'))
- gate_grad: bfloat16 [16, 768, 2048], P('expert', 'half')
- up_grad: bfloat16 [16, 768, 2048], P('expert', 'half')
- down_grad: bfloat16 [16, 768, 2048], P('expert', 'half')
The draws below stay inside these ranges and needn't reach their ends.
Inputs may be any that keep to these rules, and one draw needn't show every extreme that they name: `assign`: each row names 8 different experts. Within each aligned block of 128 rows (the rows of one index of expert) no expert is named more than 64 times, and in every draw some expert is named exactly 64 times in some block.
All inputs are finite; a program needn't handle non-finite values.
Results may differ from the reference program's by a relative error of at most 0.011.
Values may be sent and summed in bfloat16 or wider, within the bound.
No kernel may reach another device: no remote copies, remote signals or barrier semaphores. Data moves between devices by JAX's collectives and lax.ppermute only.
A program may use at most 128 MiB of HBM per device.

```python
import math
import jax
import jax.numpy as jnp
import numpy as np
from jax import lax

D = 2048
FF = 768
TOP = 8
TOK_DEV = 128
EXPERTS = 16
CAP = 64
TOKENS = 1024
N_EXPERT = 8
N_HALF = 4


def levels(own_key, shape, cuts, smallest, high):
    loudness, own = 1.0, jax.random.fold_in(own_key, 6)
    for axis_at, shards_of in cuts:
        heights = jnp.exp(jax.random.uniform(jax.random.fold_in(own, axis_at), (shards_of,), jnp.float32, smallest / len(cuts), high / len(cuts)))
        loudness = loudness * jnp.repeat(heights, shape[axis_at] // shards_of).reshape([-1 if axis == axis_at else 1 for axis in range(len(shape))])
    return loudness


def routed_block(rng, own, number, rows, number_of, top, limit, slope):
    order = jax.random.permutation(rng, number_of)
    packed, common = load_shares(number_of, rows * top, limit, slope, True), load_shares(number_of, rows * top, limit, slope, False)
    places = jnp.arange(number_of)

    def named(tallies, offset_by):
        used = int((tallies > 0).sum())
        fixed = max(1, used // 4)
        shifted = fixed + (places - fixed + offset_by * (used - fixed)) % max(1, number_of - fixed)
        return jnp.zeros((number_of,), jnp.int32).at[order[jnp.where(places < fixed, places, shifted)]].set(jnp.asarray(tallies, jnp.int32))

    tallies = jnp.where(number % 4 == 0, named(packed, number // 4), named(common, number - number // 4 - 1))
    mixed = jax.random.permutation(jax.random.fold_in(own, 3), number_of)
    giver, taker = mixed[0:number_of // 2 * 2:2], mixed[1:number_of // 2 * 2:2]
    margin = jnp.minimum(tallies[giver] - 1, limit - tallies[taker]) // 2
    margin = jnp.where((giver == order[0]) | (taker == order[0]) | (tallies[taker] == 0), 0, jnp.maximum(margin, 0))
    shifted = jax.random.randint(jax.random.fold_in(own, 4), (number_of // 2,), 0, 1 << 20) % (margin + 1)
    tallies = tallies.at[giver].add(-shifted).at[taker].add(shifted)
    items = jnp.searchsorted(jnp.cumsum(tallies), jnp.arange(rows * top), side="right").astype(jnp.int32)
    grid = items.reshape(top, rows).T
    grid = grid[jax.random.permutation(jax.random.fold_in(own, 1), rows)]
    offset_by = jax.random.randint(jax.random.fold_in(own, 2), (rows, 1), 0, top)
    return jnp.take_along_axis(grid, (jnp.arange(top)[None, :] + offset_by) % top, axis=1)


def load_shares(number_of, total, reach, skew, full):
    loads = [(1 << 20) // math.isqrt(grade ** skew) + 1 for grade in range(1, number_of + 1)]
    largest = reach if full else min(reach, max(-(-total // number_of), total * loads[0] // sum(loads)))
    least = 1 if total - largest >= number_of - 1 else 0
    given, surplus = [largest] + [least] * (number_of - 1), total - largest - least * (number_of - 1)
    while surplus > 0:
        movable = [i for i in range(1, number_of) if given[i] < largest] or [i for i in range(1, number_of) if given[i] < reach]
        mass, budget = sum([loads[i] for i in movable]), surplus
        for i in movable:
            addition = min(reach - given[i], max(1, budget * loads[i] // mass), surplus)
            given[i] = given[i] + addition
            surplus = surplus - addition
    return np.array(given)


def noise(rng, extent, deviation, reach, cuts=(), kind=jnp.bfloat16):
    array = jax.random.normal(rng, extent, jnp.float32) * deviation
    if len(cuts) > 0:
        array = levels(rng, extent, cuts, -0.22, 0.18) * array
    return jnp.clip(array, min=-reach, max=reach).astype(kind)


def setup_inputs(seed: int = 0) -> dict:
    arg_keys = jax.random.split(jax.random.key(seed), 8)
    tokens = noise(arg_keys[0], (TOKENS, D), 1.0, 6.0, ((0, 8),))
    out_grad = noise(arg_keys[1], (TOKENS, D), 1.0, 6.0, ((0, 8),))
    assign_keys = jax.random.split(jax.random.fold_in(arg_keys[2], 1), TOKENS // TOK_DEV)
    assign_turns = jax.random.permutation(jax.random.fold_in(arg_keys[2], 3), TOKENS // TOK_DEV)
    assign = jax.vmap(lambda own, number: routed_block(jax.random.fold_in(arg_keys[2], 2), own, number, TOK_DEV, EXPERTS, TOP, CAP, 2))(assign_keys, assign_turns).reshape((TOKENS, TOP))
    gate_weights = jnp.clip(0.099609375 + 0.9003906 * jax.random.uniform(arg_keys[3], (TOKENS, TOP), jnp.float32) ** levels(arg_keys[3], (TOKENS, TOP), ((0, 8),), -0.2, 0.2), 0.099609375, 1.0).astype(jnp.bfloat16)
    w_gate = noise(arg_keys[4], (EXPERTS, FF, D), D ** -0.5, 0.125, ((0, 8), (1, 4)))
    w_up = noise(arg_keys[5], (EXPERTS, FF, D), D ** -0.5, 0.125, ((0, 8), (1, 4)))
    w_down = noise(arg_keys[6], (EXPERTS, FF, D), FF ** -0.5, 0.21875, ((0, 8), (1, 4)))
    return {"tokens": tokens, "out_grad": out_grad, "assign": assign, "gate_weights": gate_weights, "w_gate": w_gate, "w_up": w_up, "w_down": w_down}


def expert_pass(rows_in, scaled, weight_gate, weight_up, weight_down):
    quarter = FF // N_HALF
    dims = (((1,), (1,)), ((), ()))
    first = (((0,), (0,)), ((), ()))
    term_sum = jnp.zeros((rows_in.shape[0], D), jnp.float32)
    gate_parts = []
    up_parts = []
    down_parts = []
    for index in range(N_HALF):
        wg_part = weight_gate[index * quarter:(index + 1) * quarter]
        wu_part = weight_up[index * quarter:(index + 1) * quarter]
        wd_part = weight_down[index * quarter:(index + 1) * quarter]
        gate_pre = lax.dot_general(rows_in, wg_part, dims, preferred_element_type=jnp.float32)
        up_pre = lax.dot_general(rows_in, wu_part, dims, preferred_element_type=jnp.float32)
        sig = jax.nn.sigmoid(gate_pre)
        silu_gate = gate_pre * sig
        hidden = (silu_gate * up_pre).astype(jnp.bfloat16)
        hidden_grad = lax.dot_general(scaled, wd_part, dims, preferred_element_type=jnp.float32)
        gate_pre_grad = (hidden_grad * up_pre * (sig * (1.0 + gate_pre * (1.0 - sig)))).astype(jnp.bfloat16)
        up_pre_grad = (hidden_grad * silu_gate).astype(jnp.bfloat16)
        down_parts.append(lax.dot_general(hidden, scaled, first, preferred_element_type=jnp.float32).astype(jnp.bfloat16))
        gate_parts.append(lax.dot_general(gate_pre_grad, rows_in, first, preferred_element_type=jnp.float32).astype(jnp.bfloat16))
        up_parts.append(lax.dot_general(up_pre_grad, rows_in, first, preferred_element_type=jnp.float32).astype(jnp.bfloat16))
        term = jnp.dot(gate_pre_grad, wg_part, preferred_element_type=jnp.float32)
        term = term + jnp.dot(up_pre_grad, wu_part, preferred_element_type=jnp.float32)
        term_sum = term_sum + term.astype(jnp.bfloat16).astype(jnp.float32)
    return (jnp.concatenate(gate_parts, 0), jnp.concatenate(up_parts, 0), jnp.concatenate(down_parts, 0), term_sum)


def reference(tokens, out_grad, assign, gate_weights, w_gate, w_up, w_down):
    pairs = TOKENS * TOP
    flat = assign.reshape(N_EXPERT, TOK_DEV * TOP)
    onehot = (flat[:, :, None] == jnp.arange(EXPERTS, dtype=jnp.int32)[None, None, :]).astype(jnp.int32)
    position = jnp.sum(jnp.cumsum(onehot, axis=1) * onehot, axis=2) - 1
    block_ids = jnp.arange(N_EXPERT, dtype=jnp.int32)[:, None]
    slot_ids = (flat * (N_EXPERT * CAP) + block_ids * CAP + position).reshape(-1).astype(jnp.int32)
    total = EXPERTS * N_EXPERT * CAP
    filler = jnp.full((total,), pairs, jnp.int32).at[slot_ids].set(jnp.arange(pairs, dtype=jnp.int32))
    filler = filler.reshape(EXPERTS, N_EXPERT * CAP)
    gate_flat = gate_weights.reshape(-1)

    def one_expert(inputs):
        fill_ids, weight_gate, weight_up, weight_down = inputs
        token_of = fill_ids // TOP
        rows_in = jnp.take(tokens, token_of, axis=0, mode="fill", fill_value=0)
        grad_rows = jnp.take(out_grad, token_of, axis=0, mode="fill", fill_value=0)
        gate_slot = jnp.take(gate_flat, fill_ids, axis=0, mode="fill", fill_value=0)
        scaled = (gate_slot.astype(jnp.float32)[:, None] * grad_rows.astype(jnp.float32)).astype(jnp.bfloat16)
        return expert_pass(rows_in, scaled, weight_gate, weight_up, weight_down)

    gate_grad, up_grad, down_grad, terms = lax.map(one_expert, (filler, w_gate, w_up, w_down))
    per_pair = jnp.take(terms.reshape(total, D), slot_ids, axis=0)
    input_grad = jnp.sum(per_pair.reshape(TOKENS, TOP, D), axis=1).astype(jnp.bfloat16)
    return input_grad, gate_grad, up_grad, down_grad
```

```python
import jax
import jax.numpy as jnp
from jax import lax
from jax.sharding import PartitionSpec as P

CAP_BASE = 12


def by_slots(tokens, out_grad, assign, gate_weights, w_gate, w_up, w_down):
    tok_rows = tokens.shape[0]
    width = tokens.shape[1]
    top_count = assign.shape[1]
    owners = lax.axis_size("expert")
    halves = lax.axis_size("half")
    exp_local = w_gate.shape[0]
    experts = owners * exp_local
    slots = slots_of(tok_rows * top_count, experts, halves)
    pairs = tok_rows * top_count
    flat = assign.reshape(-1)
    onehot = flat[:, None] == jnp.arange(experts, dtype=jnp.int32)[None, :]
    row_ids = lax.broadcasted_iota(jnp.int32, (pairs, pairs), 0)
    col_ids = lax.broadcasted_iota(jnp.int32, (pairs, pairs), 1)
    lower = (col_ids <= row_ids).astype(jnp.bfloat16)
    prefix = jnp.dot(lower, onehot.astype(jnp.bfloat16), preferred_element_type=jnp.float32)
    position = jnp.sum(prefix * onehot.astype(jnp.float32), axis=1).astype(jnp.int32) - 1
    slot_ids = flat * slots + position
    filler = (
        jnp.full((experts * slots,), pairs, jnp.int32)
        .at[slot_ids]
        .set(jnp.arange(pairs, dtype=jnp.int32))
    )
    token_of = filler // top_count
    rows_sent = jnp.take(tokens, token_of, axis=0, mode="fill", fill_value=0)
    grad_rows = jnp.take(out_grad, token_of, axis=0, mode="fill", fill_value=0)
    gate_slot = jnp.take(gate_weights.reshape(-1), filler, axis=0, mode="fill", fill_value=0)
    scaled_sent = (gate_slot.astype(jnp.float32)[:, None] * grad_rows.astype(jnp.float32)).astype(
        jnp.bfloat16
    )
    rows_sent = rows_sent.reshape(owners, exp_local, slots, width)
    scaled_sent = scaled_sent.reshape(owners, exp_local, slots, width)
    share = slots // halves
    offset = lax.axis_index("half") * share
    rows_part = lax.dynamic_slice_in_dim(rows_sent, offset, share, 2)
    scaled_part = lax.dynamic_slice_in_dim(scaled_sent, offset, share, 2)
    rows_part, scaled_part = (
        lax.all_to_all(rows_part, "expert", split_axis=0, concat_axis=0, tiled=True),
        lax.all_to_all(scaled_part, "expert", split_axis=0, concat_axis=0, tiled=True),
    )
    rows_recv, scaled_recv = (
        lax.all_gather(rows_part, "half", axis=2, tiled=True),
        lax.all_gather(scaled_part, "half", axis=2, tiled=True),
    )
    dims = (((1,), (1,)), ((), ()))
    first = (((0,), (0,)), ((), ()))
    gate_list = []
    up_list = []
    down_list = []
    term_list = []
    for local_expert in range(exp_local):
        rows_in = rows_recv[:, local_expert].reshape(owners * slots, width)
        scaled = scaled_recv[:, local_expert].reshape(owners * slots, width)
        weight_gate = w_gate[local_expert]
        weight_up = w_up[local_expert]
        weight_down = w_down[local_expert]
        gate_pre = lax.dot_general(rows_in, weight_gate, dims, preferred_element_type=jnp.float32)
        up_pre = lax.dot_general(rows_in, weight_up, dims, preferred_element_type=jnp.float32)
        sig = jax.nn.sigmoid(gate_pre)
        silu_gate = gate_pre * sig
        hidden = (silu_gate * up_pre).astype(jnp.bfloat16)
        hidden_grad = lax.dot_general(scaled, weight_down, dims, preferred_element_type=jnp.float32)
        gate_pre_grad = (hidden_grad * up_pre * (sig * (1.0 + gate_pre * (1.0 - sig)))).astype(
            jnp.bfloat16
        )
        up_pre_grad = (hidden_grad * silu_gate).astype(jnp.bfloat16)
        down_list.append(
            lax.dot_general(hidden, scaled, first, preferred_element_type=jnp.float32).astype(
                jnp.bfloat16
            )
        )
        gate_list.append(
            lax.dot_general(
                gate_pre_grad, rows_in, first, preferred_element_type=jnp.float32
            ).astype(jnp.bfloat16)
        )
        up_list.append(
            lax.dot_general(up_pre_grad, rows_in, first, preferred_element_type=jnp.float32).astype(
                jnp.bfloat16
            )
        )
        term = jnp.dot(gate_pre_grad, weight_gate, preferred_element_type=jnp.float32)
        term = term + jnp.dot(up_pre_grad, weight_up, preferred_element_type=jnp.float32)
        term_list.append(term.astype(jnp.bfloat16).reshape(owners, slots, width))
    slot_terms = jnp.stack(term_list, axis=1)
    returned = lax.all_to_all(slot_terms, "expert", split_axis=0, concat_axis=0, tiled=True)
    per_pair = jnp.take(returned.reshape(experts * slots, width), slot_ids, axis=0)
    combined = jnp.sum(per_pair.reshape(tok_rows, top_count, width).astype(jnp.float32), axis=1)
    input_grad = lax.psum_scatter(combined, "half", scatter_dimension=0, tiled=True).astype(
        jnp.bfloat16
    )
    return (input_grad, jnp.stack(gate_list, 0), jnp.stack(up_list, 0), jnp.stack(down_list, 0))

def swap(x, axis, bit):
    size = lax.axis_size(axis)
    return lax.ppermute(x, axis, [(i, i ^ (1 << bit)) for i in range(size)])


def bits_of(axis):
    return lax.axis_size(axis).bit_length() - 1


def spread(x, steps):
    for axis, bit in steps:
        x = jnp.concatenate([x, swap(x, axis, bit)], axis=0)
    return x


def fold(x, steps):
    for axis, bit in steps:
        x = (x[0].astype(jnp.float32) + swap(x[1], axis, bit).astype(jnp.float32)).astype(x.dtype)
    return x


def gathered(tokens, out_grad, assign, gate_weights, w_gate, w_up, w_down):
    tok_rows, width = tokens.shape
    owners = lax.axis_size("expert")
    halves = lax.axis_size("half")
    exp_local, units, _ = w_gate.shape
    experts = owners * exp_local
    sub = tok_rows // (2 * halves)
    me_half = lax.axis_index("half")
    me_owner = lax.axis_index("expert")
    core = me_half % 2
    side = me_half // 2
    e_low = ("expert", 0)
    e_high = [("expert", b) for b in range(bits_of("expert") - 1, 0, -1)]
    h_low = ("half", 0)
    h_high = ("half", 1)

    def piece(x, s, c, second):
        start = ((2 * s + c) * 2 + second) * sub
        return lax.dynamic_slice_in_dim(x, start, sub, 0)

    choice = assign[:, :, None] == jnp.arange(experts, dtype=jnp.int32)[None, None, :]
    share = jnp.sum(jnp.where(choice, gate_weights[:, :, None].astype(jnp.float32), 0.0), axis=1)
    share = share.astype(jnp.bfloat16)
    order = [(s, c) for c in (0, 1) for s in (0, 1)]
    share = jnp.concatenate(
        [piece(share, side ^ s, core ^ c, second) for second in (0, 1) for s, c in order], axis=0
    )
    share = spread(share[None], e_high + [e_low])
    share = share.reshape(owners, 2, 2, 2, sub, experts)

    first_t, first_g = [
        jnp.concatenate([piece(x, side, core, 0), piece(x, 1 - side, core, 0)], axis=0)
        for x in (tokens, out_grad)
    ]
    second_t, second_g = [piece(x, side, core, 1) for x in (tokens, out_grad)]
    plan_second = e_high + [e_low, h_high, h_low]
    plan_first = e_high + [e_low, h_low]
    second_t = spread(second_t, plan_second)
    second_g = spread(second_g, plan_second)
    first_t = spread(first_t, plan_first)
    first_g = spread(first_g, plan_first)

    mine = (
        jnp.arange(experts, dtype=jnp.int32)[:, None]
        == me_owner * exp_local + jnp.arange(exp_local * units, dtype=jnp.int32)[None, :] // units
    ).astype(jnp.bfloat16)
    weight_pair = jnp.concatenate(
        [w_gate.reshape(-1, width), w_up.reshape(-1, width)], axis=0
    )
    weight_down = w_down.reshape(-1, width)
    dims = (((1,), (1,)), ((), ()))
    first = (((0,), (0,)), ((), ()))
    span = exp_local * units

    def half_pass(rows_in, grads, share_rows):
        pre = lax.dot_general(rows_in, weight_pair, dims, preferred_element_type=jnp.float32)
        scale = jnp.dot(share_rows, mine, preferred_element_type=jnp.float32)
        hidden_grad = scale * lax.dot_general(
            grads, weight_down, dims, preferred_element_type=jnp.float32
        )
        gate_pre = pre[:, :span]
        up_pre = pre[:, span:]
        sig = jax.nn.sigmoid(gate_pre)
        silu_gate = gate_pre * sig
        hidden = (scale * (silu_gate * up_pre)).astype(jnp.bfloat16)
        gate_pre_grad = hidden_grad * up_pre * (sig * (1.0 + gate_pre * (1.0 - sig)))
        up_pre_grad = hidden_grad * silu_gate
        pair_grad = jnp.concatenate([gate_pre_grad, up_pre_grad], axis=1).astype(jnp.bfloat16)
        term = jnp.dot(pair_grad, weight_pair, preferred_element_type=jnp.float32)
        return hidden, pair_grad, term.astype(jnp.bfloat16)

    share_1 = share[:, 0].transpose(1, 0, 2, 3, 4).reshape(-1, experts)
    share_2 = share[:, 1].transpose(1, 2, 0, 3, 4).reshape(-1, experts)
    hid_2, pair_2, term_2 = half_pass(second_t, second_g, share_2)
    hid_1, pair_1, term_1 = half_pass(first_t, first_g, share_1)
    e_size = bits_of("expert")
    back_2 = fold(
        term_2.reshape((2, 2) + (2,) * e_size + (sub, width)), list(reversed(plan_second))
    )
    back_1 = fold(
        term_1.reshape((2,) + (2,) * e_size + (2, sub, width)), list(reversed(plan_first))
    )
    back_1 = fold(back_1, [h_high])
    input_grad = jnp.concatenate([back_1, back_2], axis=0)

    def outer(a1, b1, a2, b2):
        out = lax.dot_general(a1, b1, first, preferred_element_type=jnp.float32)
        out = out + lax.dot_general(a2, b2, first, preferred_element_type=jnp.float32)
        return out.astype(jnp.bfloat16)

    pair = outer(pair_2, second_t, pair_1, first_t)
    down = outer(hid_2, second_g, hid_1, first_g)
    pair = pair.reshape(2, exp_local, units, width)
    return input_grad, pair[0], pair[1], down.reshape(exp_local, units, width)


def on_device(tokens, out_grad, assign, gate_weights, w_gate, w_up, w_down):
    args = (tokens, out_grad, assign, gate_weights, w_gate, w_up, w_down)
    owners = lax.axis_size("expert")
    halves = lax.axis_size("half")
    tok_rows = tokens.shape[0]
    slot_rows = w_gate.shape[0] * slots_of(tok_rows * assign.shape[1], owners * w_gate.shape[0], halves)
    powers = owners & (owners - 1) == 0 and halves == 4
    if tok_rows <= slot_rows and powers:
        return gathered(*args)
    return by_slots(*args)


def slots_of(pairs, experts, halves):
    needed = (pairs + experts - 1) // experts
    return max(CAP_BASE, (needed + halves - 1) // halves * halves)


def solution(mesh):
    in_specs = (
        P("expert", None),
        P("expert", None),
        P("expert", None),
        P("expert", None),
        P("expert", "half", None),
        P("expert", "half", None),
        P("expert", "half", None),
    )
    out_specs = (
        P(("expert", "half"), None),
        P("expert", "half", None),
        P("expert", "half", None),
        P("expert", "half", None),
    )
    return jax.shard_map(
        on_device, mesh=mesh, in_specs=in_specs, out_specs=out_specs, check_vma=False
    )
```

```python
import jax
import jax.numpy as jnp
from jax import lax
from jax.sharding import PartitionSpec as P

CAP_BASE = 12


def by_slots(tokens, out_grad, assign, gate_weights, w_gate, w_up, w_down):
    tok_rows = tokens.shape[0]
    width = tokens.shape[1]
    top_count = assign.shape[1]
    owners = lax.axis_size("expert")
    halves = lax.axis_size("half")
    exp_local = w_gate.shape[0]
    experts = owners * exp_local
    slots = slots_of(tok_rows * top_count, experts, halves)
    pairs = tok_rows * top_count
    flat = assign.reshape(-1)
    onehot = flat[:, None] == jnp.arange(experts, dtype=jnp.int32)[None, :]
    row_ids = lax.broadcasted_iota(jnp.int32, (pairs, pairs), 0)
    col_ids = lax.broadcasted_iota(jnp.int32, (pairs, pairs), 1)
    lower = (col_ids <= row_ids).astype(jnp.bfloat16)
    prefix = jnp.dot(lower, onehot.astype(jnp.bfloat16), preferred_element_type=jnp.float32)
    position = jnp.sum(prefix * onehot.astype(jnp.float32), axis=1).astype(jnp.int32) - 1
    slot_ids = flat * slots + position
    filler = (
        jnp.full((experts * slots,), pairs, jnp.int32)
        .at[slot_ids]
        .set(jnp.arange(pairs, dtype=jnp.int32))
    )
    token_of = filler // top_count
    rows_sent = jnp.take(tokens, token_of, axis=0, mode="fill", fill_value=0)
    grad_rows = jnp.take(out_grad, token_of, axis=0, mode="fill", fill_value=0)
    gate_slot = jnp.take(gate_weights.reshape(-1), filler, axis=0, mode="fill", fill_value=0)
    scaled_sent = (gate_slot.astype(jnp.float32)[:, None] * grad_rows.astype(jnp.float32)).astype(
        jnp.bfloat16
    )
    rows_sent = rows_sent.reshape(owners, exp_local, slots, width)
    scaled_sent = scaled_sent.reshape(owners, exp_local, slots, width)
    share = slots // halves
    offset = lax.axis_index("half") * share
    rows_part = lax.dynamic_slice_in_dim(rows_sent, offset, share, 2)
    scaled_part = lax.dynamic_slice_in_dim(scaled_sent, offset, share, 2)
    rows_part, scaled_part = (
        lax.all_to_all(rows_part, "expert", split_axis=0, concat_axis=0, tiled=True),
        lax.all_to_all(scaled_part, "expert", split_axis=0, concat_axis=0, tiled=True),
    )
    rows_recv, scaled_recv = (
        lax.all_gather(rows_part, "half", axis=2, tiled=True),
        lax.all_gather(scaled_part, "half", axis=2, tiled=True),
    )
    dims = (((1,), (1,)), ((), ()))
    first = (((0,), (0,)), ((), ()))
    gate_list = []
    up_list = []
    down_list = []
    term_list = []
    for local_expert in range(exp_local):
        rows_in = rows_recv[:, local_expert].reshape(owners * slots, width)
        scaled = scaled_recv[:, local_expert].reshape(owners * slots, width)
        weight_gate = w_gate[local_expert]
        weight_up = w_up[local_expert]
        weight_down = w_down[local_expert]
        gate_pre = lax.dot_general(rows_in, weight_gate, dims, preferred_element_type=jnp.float32)
        up_pre = lax.dot_general(rows_in, weight_up, dims, preferred_element_type=jnp.float32)
        sig = jax.nn.sigmoid(gate_pre)
        silu_gate = gate_pre * sig
        hidden = (silu_gate * up_pre).astype(jnp.bfloat16)
        hidden_grad = lax.dot_general(scaled, weight_down, dims, preferred_element_type=jnp.float32)
        gate_pre_grad = (hidden_grad * up_pre * (sig * (1.0 + gate_pre * (1.0 - sig)))).astype(
            jnp.bfloat16
        )
        up_pre_grad = (hidden_grad * silu_gate).astype(jnp.bfloat16)
        down_list.append(
            lax.dot_general(hidden, scaled, first, preferred_element_type=jnp.float32).astype(
                jnp.bfloat16
            )
        )
        gate_list.append(
            lax.dot_general(
                gate_pre_grad, rows_in, first, preferred_element_type=jnp.float32
            ).astype(jnp.bfloat16)
        )
        up_list.append(
            lax.dot_general(up_pre_grad, rows_in, first, preferred_element_type=jnp.float32).astype(
                jnp.bfloat16
            )
        )
        term = jnp.dot(gate_pre_grad, weight_gate, preferred_element_type=jnp.float32)
        term = term + jnp.dot(up_pre_grad, weight_up, preferred_element_type=jnp.float32)
        term_list.append(term.astype(jnp.bfloat16).reshape(owners, slots, width))
    slot_terms = jnp.stack(term_list, axis=1)
    returned = lax.all_to_all(slot_terms, "expert", split_axis=0, concat_axis=0, tiled=True)
    per_pair = jnp.take(returned.reshape(experts * slots, width), slot_ids, axis=0)
    combined = jnp.sum(per_pair.reshape(tok_rows, top_count, width).astype(jnp.float32), axis=1)
    input_grad = lax.psum_scatter(combined, "half", scatter_dimension=0, tiled=True).astype(
        jnp.bfloat16
    )
    return (input_grad, jnp.stack(gate_list, 0), jnp.stack(up_list, 0), jnp.stack(down_list, 0))

def swap(x, axis, bit):
    size = lax.axis_size(axis)
    return lax.ppermute(x, axis, [(i, i ^ (1 << bit)) for i in range(size)])


def bits_of(axis):
    return lax.axis_size(axis).bit_length() - 1


def after(x, earlier):
    return lax.optimization_barrier((x, earlier))[0]


def grow(x, step):
    return jnp.concatenate([x, swap(x, *step)], axis=0)


def add(x, y):
    return (x.astype(jnp.float32) + y.astype(jnp.float32)).astype(x.dtype)


def fold(x, step):
    return add(x[0], swap(x[1], *step))


def gathered(tokens, out_grad, assign, gate_weights, w_gate, w_up, w_down):
    tok_rows, width = tokens.shape
    owners = lax.axis_size("expert")
    halves = lax.axis_size("half")
    exp_local, units, _ = w_gate.shape
    experts = owners * exp_local
    sub = tok_rows // (2 * halves)
    me_half = lax.axis_index("half")
    me_owner = lax.axis_index("expert")
    core = me_half % 2
    side = me_half // 2
    e_steps = [("expert", b) for b in range(bits_of("expert") - 1, -1, -1)]
    over_core = ("half", 0)
    over_side = ("half", 1)

    choice = assign[:, :, None] == jnp.arange(experts, dtype=jnp.int32)[None, None, :]
    share = jnp.sum(jnp.where(choice, gate_weights[:, :, None].astype(jnp.float32), 0.0), axis=1)
    pad = -experts % 128
    share = jnp.pad(share.astype(jnp.bfloat16), ((0, 0), (0, pad)))

    def piece(x, s, second):
        start = ((2 * s + core) * 2 + second) * sub
        return lax.dynamic_slice_in_dim(x, start, sub, 0)

    def packed(s, second):
        return jnp.concatenate([piece(x, s, second) for x in (tokens, out_grad, share)], axis=1)

    b_t = piece(tokens, side, 1)
    b_g = jnp.concatenate([piece(x, side, 1) for x in (out_grad, share)], axis=1)
    far = packed(1 - side, 0)
    near = packed(side, 0)

    parts = [b_t, b_g, far, near]
    first_hop = None
    grown = []
    for part in parts:
        if first_hop is not None:
            part = after(part, first_hop)
        first_hop = swap(part, *e_steps[0])
        grown.append(jnp.concatenate([part, first_hop], axis=0))
    for step in e_steps[1:]:
        grown = [grow(x, step) for x in grown]
    b_t, b_g, far, near = grown
    b_t = grow(b_t, over_side)
    b_g = grow(b_g, over_side)
    far = grow(far, over_core)
    b_t = grow(b_t, over_core)
    b_g = grow(b_g, over_core)
    near = grow(near, over_core)

    mine = (
        jnp.arange(experts + pad, dtype=jnp.int32)[:, None]
        == me_owner * exp_local + jnp.arange(exp_local * units, dtype=jnp.int32)[None, :] // units
    ).astype(jnp.bfloat16)
    weight_pair = jnp.concatenate(
        [w_gate.reshape(-1, width), w_up.reshape(-1, width)], axis=0
    )
    weight_down = w_down.reshape(-1, width)
    dims = (((1,), (1,)), ((), ()))
    first = (((0,), (0,)), ((), ()))
    span = exp_local * units

    def part_pass(rows_in, grads, share_rows):
        pre = lax.dot_general(rows_in, weight_pair, dims, preferred_element_type=jnp.float32)
        scale = jnp.dot(share_rows, mine, preferred_element_type=jnp.float32)
        hidden_grad = scale * lax.dot_general(
            grads, weight_down, dims, preferred_element_type=jnp.float32
        )
        gate_pre = pre[:, :span]
        up_pre = pre[:, span:]
        sig = jax.nn.sigmoid(gate_pre)
        silu_gate = gate_pre * sig
        hidden = (scale * (silu_gate * up_pre)).astype(jnp.bfloat16)
        gate_pre_grad = hidden_grad * up_pre * (sig * (1.0 + gate_pre * (1.0 - sig)))
        up_pre_grad = hidden_grad * silu_gate
        pair_grad = jnp.concatenate([gate_pre_grad, up_pre_grad], axis=1).astype(jnp.bfloat16)
        term = jnp.dot(pair_grad, weight_pair, preferred_element_type=jnp.float32)
        return hidden, pair_grad, term.astype(jnp.bfloat16)

    def unpack(x):
        return x[:, :width], x[:, width : 2 * width], x[:, 2 * width :]

    far_t, far_g, far_s = unpack(far)
    near_t, near_g, near_s = unpack(near)
    b_s = b_g[:, width:]
    b_g = b_g[:, :width]
    hid_f, pair_f, term_f = part_pass(far_t, far_g, far_s)
    hid_b, pair_b, term_b = part_pass(b_t, b_g, b_s)
    hid_n, pair_n, term_n = part_pass(near_t, near_g, near_s)

    twos = (2,) * bits_of("expert")
    far_sum = fold(term_f.reshape((2,) + twos + (sub, width)), over_core)
    b_sum = fold(term_b.reshape((2, 2) + twos + (sub, width)), over_core)
    b_sum = fold(jnp.moveaxis(b_sum, 1, 0), e_steps[-1])
    far_in = swap(far_sum, *over_side)
    b_sum = fold(b_sum, over_side)
    near_sum = fold(term_n.reshape((2,) + twos + (sub, width)), over_core)
    near_sum = add(near_sum, far_in)
    near_sum = fold(near_sum, e_steps[-1])
    for step in reversed(e_steps[:-1]):
        b_sum = fold(b_sum, step)
        near_sum = fold(near_sum, step)
    input_grad = jnp.concatenate([near_sum, b_sum], axis=0)

    def outer(left, right):
        out = lax.dot_general(
            jnp.concatenate(left, axis=0),
            jnp.concatenate(right, axis=0),
            first,
            preferred_element_type=jnp.float32,
        )
        return out.astype(jnp.bfloat16)

    pair = outer([pair_b, pair_f, pair_n], [b_t, far_t, near_t])
    down = outer([hid_b, hid_f, hid_n], [b_g, far_g, near_g])
    pair = pair.reshape(2, exp_local, units, width)
    return input_grad, pair[0], pair[1], down.reshape(exp_local, units, width)


def on_device(tokens, out_grad, assign, gate_weights, w_gate, w_up, w_down):
    args = (tokens, out_grad, assign, gate_weights, w_gate, w_up, w_down)
    owners = lax.axis_size("expert")
    halves = lax.axis_size("half")
    tok_rows = tokens.shape[0]
    slot_rows = w_gate.shape[0] * slots_of(tok_rows * assign.shape[1], owners * w_gate.shape[0], halves)
    powers = owners & (owners - 1) == 0 and halves == 4
    if tok_rows <= slot_rows and powers:
        return gathered(*args)
    return by_slots(*args)


def slots_of(pairs, experts, halves):
    needed = (pairs + experts - 1) // experts
    return max(CAP_BASE, (needed + halves - 1) // halves * halves)


def solution(mesh):
    in_specs = (
        P("expert", None),
        P("expert", None),
        P("expert", None),
        P("expert", None),
        P("expert", "half", None),
        P("expert", "half", None),
        P("expert", "half", None),
    )
    out_specs = (
        P(("expert", "half"), None),
        P("expert", "half", None),
        P("expert", "half", None),
        P("expert", "half", None),
    )
    return jax.shard_map(
        on_device, mesh=mesh, in_specs=in_specs, out_specs=out_specs, check_vma=False
    )
```

```python
import jax
import jax.numpy as jnp
from jax import lax
from jax.sharding import PartitionSpec as P

CAP_BASE = 12


def by_slots(tokens, out_grad, assign, gate_weights, w_gate, w_up, w_down):
    tok_rows = tokens.shape[0]
    width = tokens.shape[1]
    top_count = assign.shape[1]
    owners = lax.axis_size("expert")
    halves = lax.axis_size("half")
    exp_local = w_gate.shape[0]
    experts = owners * exp_local
    slots = slots_of(tok_rows * top_count, experts, halves)
    pairs = tok_rows * top_count
    flat = assign.reshape(-1)
    onehot = flat[:, None] == jnp.arange(experts, dtype=jnp.int32)[None, :]
    row_ids = lax.broadcasted_iota(jnp.int32, (pairs, pairs), 0)
    col_ids = lax.broadcasted_iota(jnp.int32, (pairs, pairs), 1)
    lower = (col_ids <= row_ids).astype(jnp.bfloat16)
    prefix = jnp.dot(lower, onehot.astype(jnp.bfloat16), preferred_element_type=jnp.float32)
    position = jnp.sum(prefix * onehot.astype(jnp.float32), axis=1).astype(jnp.int32) - 1
    slot_ids = flat * slots + position
    filler = (
        jnp.full((experts * slots,), pairs, jnp.int32)
        .at[slot_ids]
        .set(jnp.arange(pairs, dtype=jnp.int32))
    )
    token_of = filler // top_count
    rows_sent = jnp.take(tokens, token_of, axis=0, mode="fill", fill_value=0)
    grad_rows = jnp.take(out_grad, token_of, axis=0, mode="fill", fill_value=0)
    gate_slot = jnp.take(gate_weights.reshape(-1), filler, axis=0, mode="fill", fill_value=0)
    scaled_sent = (gate_slot.astype(jnp.float32)[:, None] * grad_rows.astype(jnp.float32)).astype(
        jnp.bfloat16
    )
    rows_sent = rows_sent.reshape(owners, exp_local, slots, width)
    scaled_sent = scaled_sent.reshape(owners, exp_local, slots, width)
    share = slots // halves
    offset = lax.axis_index("half") * share
    rows_part = lax.dynamic_slice_in_dim(rows_sent, offset, share, 2)
    scaled_part = lax.dynamic_slice_in_dim(scaled_sent, offset, share, 2)
    rows_part, scaled_part = (
        lax.all_to_all(rows_part, "expert", split_axis=0, concat_axis=0, tiled=True),
        lax.all_to_all(scaled_part, "expert", split_axis=0, concat_axis=0, tiled=True),
    )
    rows_recv, scaled_recv = (
        lax.all_gather(rows_part, "half", axis=2, tiled=True),
        lax.all_gather(scaled_part, "half", axis=2, tiled=True),
    )
    dims = (((1,), (1,)), ((), ()))
    first = (((0,), (0,)), ((), ()))
    gate_list = []
    up_list = []
    down_list = []
    term_list = []
    for local_expert in range(exp_local):
        rows_in = rows_recv[:, local_expert].reshape(owners * slots, width)
        scaled = scaled_recv[:, local_expert].reshape(owners * slots, width)
        weight_gate = w_gate[local_expert]
        weight_up = w_up[local_expert]
        weight_down = w_down[local_expert]
        gate_pre = lax.dot_general(rows_in, weight_gate, dims, preferred_element_type=jnp.float32)
        up_pre = lax.dot_general(rows_in, weight_up, dims, preferred_element_type=jnp.float32)
        sig = jax.nn.sigmoid(gate_pre)
        silu_gate = gate_pre * sig
        hidden = (silu_gate * up_pre).astype(jnp.bfloat16)
        hidden_grad = lax.dot_general(scaled, weight_down, dims, preferred_element_type=jnp.float32)
        gate_pre_grad = (hidden_grad * up_pre * (sig * (1.0 + gate_pre * (1.0 - sig)))).astype(
            jnp.bfloat16
        )
        up_pre_grad = (hidden_grad * silu_gate).astype(jnp.bfloat16)
        down_list.append(
            lax.dot_general(hidden, scaled, first, preferred_element_type=jnp.float32).astype(
                jnp.bfloat16
            )
        )
        gate_list.append(
            lax.dot_general(
                gate_pre_grad, rows_in, first, preferred_element_type=jnp.float32
            ).astype(jnp.bfloat16)
        )
        up_list.append(
            lax.dot_general(up_pre_grad, rows_in, first, preferred_element_type=jnp.float32).astype(
                jnp.bfloat16
            )
        )
        term = jnp.dot(gate_pre_grad, weight_gate, preferred_element_type=jnp.float32)
        term = term + jnp.dot(up_pre_grad, weight_up, preferred_element_type=jnp.float32)
        term_list.append(term.astype(jnp.bfloat16).reshape(owners, slots, width))
    slot_terms = jnp.stack(term_list, axis=1)
    returned = lax.all_to_all(slot_terms, "expert", split_axis=0, concat_axis=0, tiled=True)
    per_pair = jnp.take(returned.reshape(experts * slots, width), slot_ids, axis=0)
    combined = jnp.sum(per_pair.reshape(tok_rows, top_count, width).astype(jnp.float32), axis=1)
    input_grad = lax.psum_scatter(combined, "half", scatter_dimension=0, tiled=True).astype(
        jnp.bfloat16
    )
    return (input_grad, jnp.stack(gate_list, 0), jnp.stack(up_list, 0), jnp.stack(down_list, 0))

def swap(x, axis, bit):
    size = lax.axis_size(axis)
    return lax.ppermute(x, axis, [(i, i ^ (1 << bit)) for i in range(size)])


def bits_of(axis):
    return lax.axis_size(axis).bit_length() - 1


def after(x, earlier):
    return lax.optimization_barrier((x, earlier))[0]


def grow(x, step, ready=None, wait=None):
    if ready is not None:
        x = after(x, ready)
    got = swap(x, *step)
    if wait is not None:
        got = after(got, wait)
    return jnp.concatenate([x, got], axis=0), got


def add(x, y):
    return (x.astype(jnp.float32) + y.astype(jnp.float32)).astype(x.dtype)


def fold(x, labels, step, wait=None):
    at = labels.index(step)
    mine = lax.index_in_dim(x, 0, at, keepdims=False)
    got = swap(lax.index_in_dim(x, 1, at, keepdims=False), *step)
    if wait is not None:
        got = after(got, wait)
    return add(mine, got), labels[:at] + labels[at + 1 :]


def gathered(tokens, out_grad, assign, gate_weights, w_gate, w_up, w_down):
    width = tokens.shape[1]
    owners = lax.axis_size("expert")
    halves = lax.axis_size("half")
    exp_local, units, _ = w_gate.shape
    experts = owners * exp_local
    sub = tokens.shape[0] // (2 * halves)
    me_half = lax.axis_index("half")
    me_owner = lax.axis_index("expert")
    core = me_half % 2
    side = me_half // 2
    over_core = ("half", 0)
    over_side = ("half", 1)
    low = ("expert", 0)
    high = [("expert", b) for b in range(bits_of("expert") - 1, 0, -1)]

    choice = assign[:, :, None] == jnp.arange(experts, dtype=jnp.int32)[None, None, :]
    share = jnp.sum(jnp.where(choice, gate_weights[:, :, None].astype(jnp.float32), 0.0), axis=1)
    pad = -experts % 128
    share = jnp.pad(share.astype(jnp.bfloat16), ((0, 0), (0, pad)))

    def packed(s, second):
        start = ((2 * s + core) * 2 + second) * sub
        rows = [lax.dynamic_slice_in_dim(x, start, sub, 0) for x in (tokens, out_grad, share)]
        return jnp.concatenate(rows, axis=1)

    mine = (
        jnp.arange(experts + pad, dtype=jnp.int32)[:, None]
        == me_owner * exp_local + jnp.arange(exp_local * units, dtype=jnp.int32)[None, :] // units
    ).astype(jnp.bfloat16)
    weight_pair = jnp.concatenate([w_gate.reshape(-1, width), w_up.reshape(-1, width)], axis=0)
    weight_down = w_down.reshape(-1, width)
    dims = (((1,), (1,)), ((), ()))
    first = (((0,), (0,)), ((), ()))
    span = exp_local * units

    def part_pass(rows, steps, wait=None):
        rows, _ = grow(rows, over_core, wait=wait)
        steps = steps + [over_core]
        rows_in, grads, share_rows = (
            rows[:, :width],
            rows[:, width : 2 * width],
            rows[:, 2 * width :],
        )
        pre = lax.dot_general(rows_in, weight_pair, dims, preferred_element_type=jnp.float32)
        scale = jnp.dot(share_rows, mine, preferred_element_type=jnp.float32)
        hidden_grad = scale * lax.dot_general(
            grads, weight_down, dims, preferred_element_type=jnp.float32
        )
        gate_pre = pre[:, :span]
        up_pre = pre[:, span:]
        sig = jax.nn.sigmoid(gate_pre)
        silu_gate = gate_pre * sig
        hidden = (scale * (silu_gate * up_pre)).astype(jnp.bfloat16)
        gate_pre_grad = hidden_grad * up_pre * (sig * (1.0 + gate_pre * (1.0 - sig)))
        up_pre_grad = hidden_grad * silu_gate
        pair_grad = jnp.concatenate([gate_pre_grad, up_pre_grad], axis=1).astype(jnp.bfloat16)
        term = jnp.dot(pair_grad, weight_pair, preferred_element_type=jnp.float32)
        term = term.astype(jnp.bfloat16).reshape((2,) * len(steps) + (sub, width))
        term, labels = fold(term, steps[::-1], over_core)
        return (pair_grad, rows_in), (hidden, grads), term, labels

    plain = high + [low]
    turned = [low] + high
    far_1, lead = grow(packed(1 - side, 1), plain[0])
    near_1, _ = grow(packed(side, 1), turned[0])
    far_0, lead = grow(packed(1 - side, 0), plain[0], ready=lead)
    for step in plain[1:-1]:
        far_1, _ = grow(far_1, step)
    near_0, lead = grow(packed(side, 0), plain[0], ready=lead)
    for step in plain[1:-1]:
        far_0, _ = grow(far_0, step)
    far_1, landed = grow(far_1, plain[-1])
    near_1, _ = grow(near_1, turned[1], ready=lead)
    for step in plain[1:-1]:
        near_0, _ = grow(near_0, step, wait=landed)
    far_1 = part_pass(far_1, plain)
    far_0, _ = grow(far_0, plain[-1], wait=far_1[0][0])
    far_0 = part_pass(far_0, plain)
    for step in turned[2:]:
        near_1, _ = grow(near_1, step, wait=far_1[0][0])
    near_0, _ = grow(near_0, plain[-1], wait=far_0[0][0])
    near_1 = part_pass(after(near_1, far_0[0][0]), turned)
    near_0 = part_pass(near_0, plain, near_1[0][0])
    final = [low] + high[::-1]

    def aligned(x, labels):
        left = [s for s in final if s in labels]
        axes = [labels.index(s) for s in left]
        return x.transpose(axes + [x.ndim - 2, x.ndim - 1]), left

    def finish(x, labels):
        while labels:
            x, labels = fold(x, labels, [s for s in final if s in labels][0])
        return x

    near_sum = near_0[2]
    from_far_1 = swap(aligned(*far_1[2:])[0], *over_side)
    from_far_0 = swap(aligned(*far_0[2:])[0], *over_side)
    term, labels = aligned(*near_1[2:])
    done_1 = finish(*fold(add(term, from_far_1), labels, low, near_sum))
    term, labels = aligned(*near_0[2:])
    done_0 = finish(add(term, from_far_0), labels)
    input_grad = jnp.concatenate([done_0, done_1], axis=0)

    def outer(at):
        left, right = zip(*[part[at] for part in (far_0, far_1, near_0, near_1)])
        left, right = after((left, right), near_sum)
        out = lax.dot_general(
            jnp.concatenate(left, axis=0),
            jnp.concatenate(right, axis=0),
            first,
            preferred_element_type=jnp.float32,
        )
        return out.astype(jnp.bfloat16)

    pair = outer(0).reshape(2, exp_local, units, width)
    down = outer(1).reshape(exp_local, units, width)
    return input_grad, pair[0], pair[1], down


def on_device(tokens, out_grad, assign, gate_weights, w_gate, w_up, w_down):
    args = (tokens, out_grad, assign, gate_weights, w_gate, w_up, w_down)
    owners = lax.axis_size("expert")
    halves = lax.axis_size("half")
    tok_rows = tokens.shape[0]
    slot_rows = w_gate.shape[0] * slots_of(tok_rows * assign.shape[1], owners * w_gate.shape[0], halves)
    powers = owners & (owners - 1) == 0 and halves == 4
    if tok_rows <= slot_rows and powers:
        return gathered(*args)
    return by_slots(*args)


def slots_of(pairs, experts, halves):
    needed = (pairs + experts - 1) // experts
    return max(CAP_BASE, (needed + halves - 1) // halves * halves)


def solution(mesh):
    in_specs = (
        P("expert", None),
        P("expert", None),
        P("expert", None),
        P("expert", None),
        P("expert", "half", None),
        P("expert", "half", None),
        P("expert", "half", None),
    )
    out_specs = (
        P(("expert", "half"), None),
        P("expert", "half", None),
        P("expert", "half", None),
        P("expert", "half", None),
    )
    return jax.shard_map(
        on_device, mesh=mesh, in_specs=in_specs, out_specs=out_specs, check_vma=False
    )
```
